32 devices in a mesh: wave: 8 (over y, x, core), lev: 4 (over z).
Axes of the slice: x: 2, y: 2, z: 4, core: 2. Of those that a mesh axis runs over, the one named last changes fastest.
Arguments:
- coefficients: bfloat16 [640, 640, 512], P('wave', 'lev'), may hold values from -6 to 6
- factors: bfloat16 [3, 2, 640, 80, 640], P(None, None, 'wave', None, 'lev'), may hold values from -0.5 to 0.5
- wave_ids: int32 [640], replicated, may hold values from 0 to 639, each once
Outputs:
- grid: bfloat16 [640, 256, 2560], P(('wave', 'lev'))
The draws below stay inside these ranges and needn't reach their ends.
Inputs may be any that keep to these rules, and one draw needn't show every extreme that they name: `wave_ids`: each wavenumber 0 .. 639 appears exactly once.
All inputs are finite; a program needn't handle non-finite values.
Results may differ from the reference program's by a relative error of at most 0.0079.
Values may be sent and summed in bfloat16 or wider, within the bound.
A program may use at most 192 MiB of HBM per device.

```python
import math
import jax
import jax.numpy as jnp
from jax import lax

NDEG = 640
WAVES = 640
NLON = 2560
FIELDS = 8
LEVELS = 32
SECTIONS = 3
N_WAVE = 8
N_LEV = 4


def block_scale(rng, extent, shards, least, largest):
    gain = 1.0
    for position, shards_of in shards:
        draws = jax.random.uniform(jax.random.fold_in(jax.random.fold_in(rng, 6), position), (shards_of,), jnp.float32, least / len(shards), largest / len(shards))
        gain = gain * jnp.repeat(jnp.exp(draws), extent[position] // shards_of).reshape((-1,) + (1,) * (len(extent) - 1 - position))
    return gain


def noise(own_key, dims, scale, reach, cuts=(), held_as=jnp.bfloat16):
    array = jax.random.normal(own_key, dims, jnp.float32) * scale
    if len(cuts) > 0:
        array = block_scale(own_key, dims, cuts, -0.22, 0.18) * array
    return jnp.clip(array, min=-reach, max=reach).astype(held_as)


def setup_inputs(seed: int = 0) -> dict:
    arg_keys = jax.random.split(jax.random.key(seed), 4)
    return {
        "coefficients": noise(arg_keys[0], (NDEG, WAVES, 2 * FIELDS * LEVELS), 1.0, 6.0, ((0, 8), (1, 4))),
        "factors": noise(arg_keys[1], (SECTIONS, 2, NDEG, NDEG // N_WAVE, WAVES), (2 * NDEG // N_WAVE) ** -0.5, 0.5, ((2, 8), (4, 4))),
        "wave_ids": jax.random.permutation(arg_keys[2], WAVES).astype(jnp.int32),
    }


def reference(coefficients, factors, wave_ids):
    deg_block = NDEG // N_WAVE
    wave_block = WAVES // N_LEV
    channels = 2 * FIELDS * LEVELS
    degree = jnp.arange(NDEG, dtype=jnp.int32)

    def synthesize(block_index):
        offset = (block_index * wave_block).astype(jnp.int32)
        coef_block = lax.dynamic_slice_in_dim(coefficients, offset, wave_block, 1)
        own_ids = lax.dynamic_slice_in_dim(wave_ids, offset, wave_block, 0)
        live_mask = (degree[:, None] >= own_ids[None, :])[:, :, None]
        current = jnp.where(live_mask, coef_block, jnp.zeros((), coefficients.dtype))
        for section in range(SECTIONS):
            stride = 1 << section
            section_factors = lax.dynamic_slice_in_dim(factors[section], offset, wave_block, 3).astype(jnp.float32)
            self_factor = section_factors[0].reshape(N_WAVE, deg_block, deg_block, wave_block)
            partner_factor = section_factors[1].reshape(N_WAVE, deg_block, deg_block, wave_block)
            blocks_now = current.astype(jnp.float32).reshape(N_WAVE, deg_block, wave_block, channels)
            partner = blocks_now.reshape(N_WAVE // (2 * stride), 2, stride, deg_block, wave_block, channels)[:, ::-1]
            partner = partner.reshape(blocks_now.shape)
            combined = jnp.einsum('woim,wimc->womc', self_factor, blocks_now)
            combined = combined + jnp.einsum('woim,wimc->womc', partner_factor, partner)
            current = combined.reshape(NDEG, wave_block, channels).astype(jnp.bfloat16)
        return current
    blocks = lax.map(synthesize, jnp.arange(N_LEV, dtype=jnp.int32))
    lat_rows = jnp.transpose(blocks, (1, 0, 2, 3)).reshape(NDEG, WAVES, 2, FIELDS * LEVELS)
    longitude = jnp.arange(NLON, dtype=jnp.int32)
    phases = wave_ids[:, None] * longitude[None, :] % NLON
    angles = phases.astype(jnp.float32) * (2.0 * math.pi / NLON)
    weight = jnp.where(wave_ids == 0, 1.0, 2.0).astype(jnp.float32) / math.sqrt(2.0 * WAVES)
    cosine_part = weight[:, None] * jnp.cos(angles)
    sine_part = -weight[:, None] * jnp.sin(angles)
    fourier_table = jnp.stack([cosine_part, sine_part], axis=1).astype(jnp.bfloat16).astype(jnp.float32)
    lat_block = math.gcd(NDEG, 64)

    def fourier(block_index):
        offset = (block_index * lat_block).astype(jnp.int32)
        piece = lax.dynamic_slice_in_dim(lat_rows, offset, lat_block, 0).astype(jnp.float32)
        return jnp.einsum('rmpc,mpj->rcj', piece, fourier_table).astype(jnp.bfloat16)
    grid = lax.map(fourier, jnp.arange(NDEG // lat_block, dtype=jnp.int32))
    return grid.reshape(NDEG, FIELDS * LEVELS, NLON)
```

```python
import functools
import math

import jax
import jax.numpy as jnp
from jax import lax
from jax.experimental import pallas as pl
from jax.experimental.pallas import tpu as pltpu
from jax.sharding import PartitionSpec as P


NLON = 2560
UNIT = 16


def swapped(block, axis, apart):
    count = lax.axis_size(axis)
    route = []
    for low in range(count):
        high = low | 1 << apart
        if high != low and high < count:
            route += [(low, high), (high, low)]
    return lax.ppermute(block, axis, route)


def combine_kernel(count, factor_ref, own_ref, partner_ref, *refs):
    out_ref = refs[-1]
    for m in range(count):
        total = jnp.dot(factor_ref[0, m], own_ref[m], preferred_element_type=jnp.float32)
        total += jnp.dot(factor_ref[1, m], partner_ref[m], preferred_element_type=jnp.float32)
        out_ref[m] = total.astype(out_ref.dtype)


def combine(factor, own, partner, start, after):
    slots, rows, channels = own.shape
    step = math.gcd(slots, 8)
    block = pl.BlockSpec((step, rows, channels), lambda i: (i, 0, 0))
    return pl.pallas_call(
        functools.partial(combine_kernel, step),
        grid=(slots // step,),
        out_shape=jax.ShapeDtypeStruct(own.shape, own.dtype),
        in_specs=[
            pl.BlockSpec((2, step, rows, rows), lambda i: (0, start // step + i, 0, 0)),
            block,
            block,
        ]
        + [pl.BlockSpec(memory_space=pl.ANY)] * len(after),
        out_specs=block,
        cost_estimate=pl.CostEstimate(
            flops=4 * slots * rows * rows * channels,
            bytes_accessed=2 * (3 * own.size + 2 * slots * rows * rows),
            transcendentals=0,
        ),
    )(factor, own, partner, *after)


def synthesis_kernel(count, *refs):
    table_ref, out_ref = refs[count], refs[count + 1]
    half = out_ref.shape[1]
    wide = jnp.concatenate([ref[0] for ref in refs[:count]], axis=0)
    turned = wide.T
    spectrum = jnp.concatenate([turned[:half], turned[half:]], axis=1)
    span = math.gcd(out_ref.shape[2], 512)
    for j in range(0, out_ref.shape[2], span):
        out_ref[0, :, j : j + span] = jnp.dot(
            spectrum, table_ref[:, j : j + span], preferred_element_type=jnp.float32
        ).astype(out_ref.dtype)


def synthesis(parts, table):
    rows, _, channels = parts[0].shape
    depth, longitudes = table.shape
    return pl.pallas_call(
        functools.partial(synthesis_kernel, len(parts)),
        grid=(rows,),
        out_shape=jax.ShapeDtypeStruct((rows, channels // 2, longitudes), parts[0].dtype),
        in_specs=[pl.BlockSpec((1, p.shape[1], channels), lambda i: (i, 0, 0)) for p in parts]
        + [pl.BlockSpec((depth, longitudes), lambda i: (0, 0), pipeline_mode=pl.Buffered(1))],
        out_specs=pl.BlockSpec((1, channels // 2, longitudes), lambda i: (i, 0, 0)),
        cost_estimate=pl.CostEstimate(
            flops=rows * channels * depth * longitudes,
            bytes_accessed=rows * channels * (depth + longitudes) + 2 * table.size,
            transcendentals=0,
        ),
    )(*parts, table)


def cuts_of(slots):
    unit = math.gcd(slots, 16)
    edges = [0]
    while edges[-1] < slots:
        left = slots - edges[-1]
        edges.append(edges[-1] + (unit if edges[-1] == 0 or left <= 2 * unit else 2 * unit))
    return list(zip(edges[:-1], edges[1:]))


def mixes(pieces, sections):
    return [
        (t - s - (s > 0), s)
        for t in range(pieces + sections + 1)
        for s in range(sections)
        if 0 <= t - s - (s > 0) < pieces
    ]


def body(coefficients, factors, wave_ids):
    wave_count = lax.axis_size("wave")
    lev_count = lax.axis_size("lev")
    sections = wave_count.bit_length() - 1
    rows, slots, _ = coefficients.shape
    total_waves = wave_ids.shape[0]
    wave_pos = lax.axis_index("wave")
    lev_pos = lax.axis_index("lev")
    cuts = cuts_of(slots)
    pieces = len(cuts)
    band = rows // lev_count
    ids = [
        lax.dynamic_slice_in_dim(wave_ids, (lev_pos - d) % lev_count * slots, slots, 0)
        for d in range(lev_count)
    ]
    degree = wave_pos * rows + jnp.arange(rows, dtype=jnp.int32)
    factor = [factors[s].transpose(0, 3, 1, 2) for s in range(sections)]

    current = [None] * pieces
    gathered = [None] * pieces

    def start(c):
        low, high = cuts[c]
        live = (degree[:, None] >= ids[0][low:high][None, :])[:, :, None]
        block = coefficients[:, low:high, :]
        block = jnp.where(live, block, jnp.zeros((), block.dtype))
        return block.transpose(1, 0, 2)

    def spread(c):
        ready = current[c].transpose(1, 0, 2)
        got = [lax.dynamic_slice_in_dim(ready, lev_pos * band, band, 0)]
        for d in range(1, lev_count):
            part = lax.dynamic_slice_in_dim(ready, (lev_pos + d) % lev_count * band, band, 0)
            route = [(k, (k + d) % lev_count) for k in range(lev_count)]
            got.append(lax.ppermute(part, "lev", route))
        gathered[c] = got

    for c in range(pieces):
        current[c] = start(c)
    after = []
    for c, s in mixes(pieces, sections):
        partner = swapped(current[c], "wave", s)
        current[c] = combine(factor[s], current[c], partner, cuts[c][0], after)
        after = [current[c]]
        if s == sections - 1:
            spread(c)

    table_ids = jnp.concatenate([ids[d][low:high] for low, high in cuts for d in range(lev_count)])
    longitude = jnp.arange(NLON, dtype=jnp.int32)
    phases = table_ids[:, None] * longitude[None, :] % NLON
    angles = phases.astype(jnp.float32) * (2.0 * math.pi / NLON)
    weight = jnp.where(table_ids == 0, 1.0, 2.0).astype(jnp.float32) / math.sqrt(2.0 * total_waves)
    cosine_part = (weight[:, None] * jnp.cos(angles)).astype(jnp.bfloat16)
    sine_part = (-weight[:, None] * jnp.sin(angles)).astype(jnp.bfloat16)
    table = jnp.concatenate([cosine_part, sine_part], axis=0)

    return synthesis([part for got in gathered for part in got], table)


def whole(coefficients, factors, wave_ids):
    return body(coefficients, factors, wave_ids)


MESH = pl.DeviceIdType.MESH
RING = 3


def exchange_kernel(
    unit,
    ids_ref,
    coef_ref,
    factor_ref,
    bands_ref,
    coef_in,
    factor_in,
    factor_f32,
    factor,
    turn,
    mixed,
    ready,
    coef_sem,
    factor_sem,
    send_sem,
    recv_sem,
    band_send,
    band_recv,
    band_own,
    free_sem,
):
    wave_pos, lev_pos = lax.axis_index("wave"), lax.axis_index("lev")
    lev_count = lax.axis_size("lev")
    rows, slots, channels = coef_ref.shape
    sections = factor_ref.shape[0]
    chunks = slots // unit
    band = rows // lev_count
    group = factor_in.shape[2]
    groups = rows // group
    jobs = sections * groups
    lane = 128

    def other(s):
        bit = 1 << s
        return jnp.where(wave_pos // bit % 2 == 0, wave_pos + bit, wave_pos - bit)

    def peer(d):
        return lax.rem(lev_pos + d, lev_count)

    barrier = pltpu.get_barrier_semaphore()
    for s in range(sections):
        pl.semaphore_signal(barrier, inc=1, device_id={"wave": other(s)}, device_id_type=MESH)
    for d in range(1, lev_count):
        pl.semaphore_signal(barrier, inc=1, device_id={"lev": peer(d)}, device_id_type=MESH)

    def coef_copy(c):
        k = lax.rem(c, 2)
        return pltpu.make_async_copy(
            coef_ref.at[:, pl.ds(pl.multiple_of(c * unit, unit), unit), :], coef_in.at[k], coef_sem.at[k]
        )

    def factor_copy(j):
        k = lax.rem(j, 2)
        s, g = lax.div(j, groups), lax.rem(j, groups)
        return pltpu.make_async_copy(
            factor_ref.at[s, :, pl.ds(g * group, group)], factor_in.at[k], factor_sem.at[k]
        )

    for k in range(2):
        coef_copy(k).start()
        factor_copy(k).start()

    def slot(s, c):
        return s * RING + lax.rem(c, RING)

    def swap(s, c):
        k = slot(s, c)
        return pltpu.make_async_remote_copy(
            src_ref=mixed.at[k, :, pl.ds(0, rows), :],
            dst_ref=mixed.at[k, :, pl.ds(rows, rows), :],
            send_sem=send_sem.at[k],
            recv_sem=recv_sem.at[k],
            device_id={"wave": other(s)},
            device_id_type=MESH,
        )

    def band_copy(d, c, owner):
        k = lax.rem(c, RING)
        return pltpu.make_async_remote_copy(
            src_ref=ready.at[k, pl.ds(peer(d) * band, band)],
            dst_ref=bands_ref.at[:, pl.ds(pl.multiple_of(owner * slots + c * unit, unit), unit), :],
            send_sem=band_send.at[k, d - 1],
            recv_sem=band_recv.at[c, d - 1],
            device_id={"lev": peer(d)},
            device_id_type=MESH,
        )

    def own_copy(c):
        k = lax.rem(c, RING)
        return pltpu.make_async_copy(
            ready.at[k, pl.ds(lev_pos * band, band)],
            bands_ref.at[:, pl.ds(pl.multiple_of(lev_pos * slots + c * unit, unit), unit), :],
            band_own.at[k],
        )

    def release(s, c):
        @pl.when(c >= RING)
        def _():
            swap(s, c - RING).wait_send()

    def send(s, c):
        @pl.when(c >= RING)
        def _():
            pl.semaphore_wait(free_sem.at[s], 1)

        swap(s, c).start()

    degree = wave_pos * rows + lax.broadcasted_iota(jnp.int32, (rows, lane), 0)

    def begin(c):
        coef_copy(c).wait()
        for n, low in enumerate(range(0, channels, lane)):
            part = coef_in[lax.rem(c, 2), :, :, pl.ds(low, lane)].astype(jnp.float32)
            turn[n] = part.reshape(rows * unit, lane)

        @pl.when(c + 2 < chunks)
        def _():
            coef_copy(c + 2).start()

        release(0, c)
        k = slot(0, c)
        for m in range(unit):
            live = degree >= ids_ref[pl.ds(c * unit + m, 1), :]
            for n, low in enumerate(range(0, channels, lane)):
                part = turn[n, pl.ds(m, rows, stride=unit), :]
                part = jnp.where(live, part, 0.0)
                mixed[k, m, pl.ds(0, rows), pl.ds(low, lane)] = part.astype(mixed.dtype)
        send(0, c)

    def prepare(s):
        def job(g, carry):
            j = s * groups + g
            factor_copy(j).wait()
            k = lax.rem(j, 2)
            for o in range(group):
                both = jnp.concatenate([factor_in[k, 0, o], factor_in[k, 1, o]], axis=0)
                rest = jnp.zeros((2 * lane - 2 * rows, slots), both.dtype)
                for n, part in enumerate((both[:lane], jnp.concatenate([both[lane:], rest], axis=0))):
                    factor_f32[n, pl.ds(o, slots, stride=group), :] = part.T.astype(jnp.float32)

            @pl.when(j + 2 < jobs)
            def _():
                factor_copy(j + 2).start()

            low = pl.multiple_of(g * group, group)
            for n in range(2):
                factor[pl.ds(s * slots, slots), pl.ds(low, group), pl.ds(n * lane, lane)] = (
                    factor_f32[n].astype(factor.dtype).reshape(slots, group, lane)
                )
            return carry

        lax.fori_loop(0, groups, job, 0)

    def mix(s, c):
        k = slot(s, c)
        swap(s, c).wait_recv()
        last = s == sections - 1
        if last:

            @pl.when(c >= RING)
            def _():
                for d in range(1, lev_count):
                    band_copy(d, c - RING, lev_pos).wait_send()
                own_copy(c - RING).wait()

        else:
            release(s + 1, c)
        for m in range(unit):
            total = jnp.dot(
                factor[s * slots + c * unit + m][:, : 2 * rows], mixed[k, m], preferred_element_type=jnp.float32
            )
            if last:
                for n, low in enumerate(range(0, channels, lane)):
                    turn[n, pl.ds(m, rows, stride=unit), :] = total[:, low : low + lane]
            else:
                mixed[slot(s + 1, c), m, pl.ds(0, rows), :] = total.astype(mixed.dtype)

        @pl.when(c < chunks - RING)
        def _():
            pl.semaphore_signal(free_sem.at[s], inc=1, device_id={"wave": other(s)}, device_id_type=MESH)

        if last:
            for n, low in enumerate(range(0, channels, lane)):
                ready[lax.rem(c, RING), :, :, pl.ds(low, lane)] = (
                    turn[n].astype(ready.dtype).reshape(rows, unit, lane)
                )
            for d in (lev_count // 2, 1, lev_count - 1) if lev_count == 4 else range(1, lev_count):
                band_copy(d, c, lev_pos).start()
            own_copy(c).start()
        else:
            send(s + 1, c)

    def guarded(s, c):
        @pl.when((c >= 0) & (c < chunks))
        def _():
            mix(s, c)

    pl.semaphore_wait(barrier, sections + lev_count - 1)

    def step(t, carry):
        guarded(0, t - 1)

        @pl.when(t < chunks)
        def _():
            begin(t)

        for s in range(1, sections - 1):
            guarded(s, t - 1 - s)

        @pl.when(t < sections)
        def _():
            prepare(t)

        guarded(sections - 1, t - sections)
        return carry

    lax.fori_loop(0, chunks + sections, step, 0)

    for c in range(chunks - RING, chunks):
        for s in range(sections):
            swap(s, jnp.int32(c)).wait_send()
        for d in range(1, lev_count):
            band_copy(d, jnp.int32(c), lev_pos).wait_send()
        own_copy(jnp.int32(c)).wait()

    def arrived(c, carry):
        for d in range(1, lev_count):
            band_copy(d, c, peer(lev_count - d)).wait_recv()
        return carry

    lax.fori_loop(0, chunks, arrived, 0)


def exchange(ids, coefficients, factors, unit):
    lev_count = lax.axis_size("lev")
    rows, slots, channels = coefficients.shape
    sections = factors.shape[0]
    chunks = slots // unit
    kind = coefficients.dtype
    group = 16
    return pl.pallas_call(
        functools.partial(exchange_kernel, unit),
        out_shape=jax.ShapeDtypeStruct((rows // lev_count, lev_count * slots, channels), kind),
        in_specs=[
            pl.BlockSpec(memory_space=pltpu.VMEM),
            pl.BlockSpec(memory_space=pltpu.HBM),
            pl.BlockSpec(memory_space=pltpu.HBM),
        ],
        out_specs=pl.BlockSpec(memory_space=pltpu.HBM),
        scratch_shapes=[
            pltpu.VMEM((2, rows, unit, channels), kind),
            pltpu.VMEM((2, 2, group, rows, slots), kind),
            pltpu.VMEM((2, slots * group, 128), jnp.float32),
            pltpu.VMEM((sections * slots, rows, 256), kind),
            pltpu.VMEM((channels // 128, rows * unit, 128), jnp.float32),
            pltpu.VMEM((sections * RING, unit, 2 * rows, channels), kind),
            pltpu.VMEM((RING, rows, unit, channels), kind),
            pltpu.SemaphoreType.DMA((2,)),
            pltpu.SemaphoreType.DMA((2,)),
            pltpu.SemaphoreType.DMA((sections * RING,)),
            pltpu.SemaphoreType.DMA((sections * RING,)),
            pltpu.SemaphoreType.DMA((RING, lev_count - 1)),
            pltpu.SemaphoreType.DMA((chunks, lev_count - 1)),
            pltpu.SemaphoreType.DMA((RING,)),
            pltpu.SemaphoreType.REGULAR((sections,)),
        ],
        compiler_params=pltpu.CompilerParams(
            collective_id=0, has_side_effects=True, vmem_limit_bytes=60 << 20
        ),
    )(ids, coefficients, factors)


def grid_kernel(cos_a, sin_a, cos_b, sin_b, u_ref, out_ref, table):
    slots = cos_a.shape[0]
    half = out_ref.shape[1]
    lane = cos_b.shape[1]

    @pl.when(pl.program_id(0) == 0)
    def _():
        for j in range(out_ref.shape[2] // lane):
            ca, sa = cos_a[:, j : j + 1], sin_a[:, j : j + 1]
            table[:slots, j * lane : (j + 1) * lane] = (ca * cos_b[...] - sa * sin_b[...]).astype(table.dtype)
            table[slots:, j * lane : (j + 1) * lane] = (-(sa * cos_b[...] + ca * sin_b[...])).astype(table.dtype)

    turned = u_ref[0].T
    spectrum = jnp.concatenate([turned[:half], turned[half:]], axis=1)
    span = math.gcd(out_ref.shape[2], 512)
    for j in range(0, out_ref.shape[2], span):
        out_ref[0, :, j : j + span] = jnp.dot(
            spectrum, table[:, j : j + span], preferred_element_type=jnp.float32
        ).astype(out_ref.dtype)


def grid_of(wave_ids, bands):
    rows, slots, channels = bands.shape
    lane = 128

    def angle(j):
        phases = wave_ids[:, None] * j[None, :] % NLON
        return phases.astype(jnp.float32) * (2.0 * math.pi / NLON)

    weight = jnp.where(wave_ids == 0, 1.0, 2.0).astype(jnp.float32) / math.sqrt(2.0 * wave_ids.shape[0])
    a = angle(lane * jnp.arange(NLON // lane, dtype=jnp.int32))
    b = angle(jnp.arange(lane, dtype=jnp.int32))
    parts = [weight[:, None] * jnp.cos(a), weight[:, None] * jnp.sin(a), jnp.cos(b), jnp.sin(b)]
    return pl.pallas_call(
        grid_kernel,
        grid=(rows,),
        out_shape=jax.ShapeDtypeStruct((rows, channels // 2, NLON), bands.dtype),
        in_specs=[pl.BlockSpec(p.shape, lambda i: (0, 0), pipeline_mode=pl.Buffered(1)) for p in parts]
        + [pl.BlockSpec((1, slots, channels), lambda i: (i, 0, 0))],
        out_specs=pl.BlockSpec((1, channels // 2, NLON), lambda i: (i, 0, 0)),
        scratch_shapes=[pltpu.VMEM((2 * slots, NLON), bands.dtype)],
        cost_estimate=pl.CostEstimate(
            flops=2 * rows * channels * slots * NLON,
            bytes_accessed=2 * bands.size + rows * channels * NLON,
            transcendentals=0,
        ),
    )(*parts, bands)


def unit_of(rows, slots):
    return UNIT if rows % 16 == 0 and 128 <= 2 * rows <= 256 and slots % UNIT == 0 and slots // UNIT > RING else 0


def staged(coefficients, factors, wave_ids):
    rows, slots, _ = coefficients.shape
    ids = lax.dynamic_slice_in_dim(wave_ids, lax.axis_index("lev") * slots, slots, 0)
    ids = jnp.broadcast_to(ids[:, None], (slots, 128))
    bands = exchange(ids, coefficients, factors, unit_of(rows, slots))
    return grid_of(wave_ids, bands)


def solution(mesh):
    in_specs = (P("wave", "lev", None), P(None, None, "wave", None, "lev"), P())
    out_specs = P(("wave", "lev"), None, None)

    def mapped(step):
        return jax.shard_map(step, mesh=mesh, in_specs=in_specs, out_specs=out_specs, check_vma=False)

    def run(coefficients, factors, wave_ids):
        lev_count = mesh.shape["lev"]
        slots = coefficients.shape[1] // lev_count
        if unit_of(factors.shape[3], slots):
            return mapped(staged)(coefficients, factors, wave_ids)
        return mapped(whole)(coefficients, factors, wave_ids)

    return run
```

```python
import functools
import math

import jax
import jax.numpy as jnp
from jax import lax
from jax.experimental import pallas as pl
from jax.experimental.pallas import tpu as pltpu
from jax.sharding import PartitionSpec as P


NLON = 2560
UNIT = 8
SPLIT = 2
EARLY = 12


def swapped(block, axis, apart):
    count = lax.axis_size(axis)
    route = []
    for low in range(count):
        high = low | 1 << apart
        if high != low and high < count:
            route += [(low, high), (high, low)]
    return lax.ppermute(block, axis, route)


def combine_kernel(count, factor_ref, own_ref, partner_ref, *refs):
    out_ref = refs[-1]
    for m in range(count):
        total = jnp.dot(factor_ref[0, m], own_ref[m], preferred_element_type=jnp.float32)
        total += jnp.dot(factor_ref[1, m], partner_ref[m], preferred_element_type=jnp.float32)
        out_ref[m] = total.astype(out_ref.dtype)


def combine(factor, own, partner, start, after):
    slots, rows, channels = own.shape
    step = math.gcd(slots, 8)
    block = pl.BlockSpec((step, rows, channels), lambda i: (i, 0, 0))
    return pl.pallas_call(
        functools.partial(combine_kernel, step),
        grid=(slots // step,),
        out_shape=jax.ShapeDtypeStruct(own.shape, own.dtype),
        in_specs=[
            pl.BlockSpec((2, step, rows, rows), lambda i: (0, start // step + i, 0, 0)),
            block,
            block,
        ]
        + [pl.BlockSpec(memory_space=pl.ANY)] * len(after),
        out_specs=block,
        cost_estimate=pl.CostEstimate(
            flops=4 * slots * rows * rows * channels,
            bytes_accessed=2 * (3 * own.size + 2 * slots * rows * rows),
            transcendentals=0,
        ),
    )(factor, own, partner, *after)


def synthesis_kernel(count, *refs):
    table_ref, out_ref = refs[count], refs[count + 1]
    half = out_ref.shape[1]
    wide = jnp.concatenate([ref[0] for ref in refs[:count]], axis=0)
    turned = wide.T
    spectrum = jnp.concatenate([turned[:half], turned[half:]], axis=1)
    span = math.gcd(out_ref.shape[2], 512)
    for j in range(0, out_ref.shape[2], span):
        out_ref[0, :, j : j + span] = jnp.dot(
            spectrum, table_ref[:, j : j + span], preferred_element_type=jnp.float32
        ).astype(out_ref.dtype)


def synthesis(parts, table):
    rows, _, channels = parts[0].shape
    depth, longitudes = table.shape
    return pl.pallas_call(
        functools.partial(synthesis_kernel, len(parts)),
        grid=(rows,),
        out_shape=jax.ShapeDtypeStruct((rows, channels // 2, longitudes), parts[0].dtype),
        in_specs=[pl.BlockSpec((1, p.shape[1], channels), lambda i: (i, 0, 0)) for p in parts]
        + [pl.BlockSpec((depth, longitudes), lambda i: (0, 0), pipeline_mode=pl.Buffered(1))],
        out_specs=pl.BlockSpec((1, channels // 2, longitudes), lambda i: (i, 0, 0)),
        cost_estimate=pl.CostEstimate(
            flops=rows * channels * depth * longitudes,
            bytes_accessed=rows * channels * (depth + longitudes) + 2 * table.size,
            transcendentals=0,
        ),
    )(*parts, table)


def cuts_of(slots):
    unit = math.gcd(slots, 16)
    edges = [0]
    while edges[-1] < slots:
        left = slots - edges[-1]
        edges.append(edges[-1] + (unit if edges[-1] == 0 or left <= 2 * unit else 2 * unit))
    return list(zip(edges[:-1], edges[1:]))


def mixes(pieces, sections):
    return [
        (t - s - (s > 0), s)
        for t in range(pieces + sections + 1)
        for s in range(sections)
        if 0 <= t - s - (s > 0) < pieces
    ]


def body(coefficients, factors, wave_ids):
    wave_count = lax.axis_size("wave")
    lev_count = lax.axis_size("lev")
    sections = wave_count.bit_length() - 1
    rows, slots, _ = coefficients.shape
    total_waves = wave_ids.shape[0]
    wave_pos = lax.axis_index("wave")
    lev_pos = lax.axis_index("lev")
    cuts = cuts_of(slots)
    pieces = len(cuts)
    band = rows // lev_count
    ids = [
        lax.dynamic_slice_in_dim(wave_ids, (lev_pos - d) % lev_count * slots, slots, 0)
        for d in range(lev_count)
    ]
    degree = wave_pos * rows + jnp.arange(rows, dtype=jnp.int32)
    factor = [factors[s].transpose(0, 3, 1, 2) for s in range(sections)]

    current = [None] * pieces
    gathered = [None] * pieces

    def start(c):
        low, high = cuts[c]
        live = (degree[:, None] >= ids[0][low:high][None, :])[:, :, None]
        block = coefficients[:, low:high, :]
        block = jnp.where(live, block, jnp.zeros((), block.dtype))
        return block.transpose(1, 0, 2)

    def spread(c):
        ready = current[c].transpose(1, 0, 2)
        got = [lax.dynamic_slice_in_dim(ready, lev_pos * band, band, 0)]
        for d in range(1, lev_count):
            part = lax.dynamic_slice_in_dim(ready, (lev_pos + d) % lev_count * band, band, 0)
            route = [(k, (k + d) % lev_count) for k in range(lev_count)]
            got.append(lax.ppermute(part, "lev", route))
        gathered[c] = got

    for c in range(pieces):
        current[c] = start(c)
    after = []
    for c, s in mixes(pieces, sections):
        partner = swapped(current[c], "wave", s)
        current[c] = combine(factor[s], current[c], partner, cuts[c][0], after)
        after = [current[c]]
        if s == sections - 1:
            spread(c)

    table_ids = jnp.concatenate([ids[d][low:high] for low, high in cuts for d in range(lev_count)])
    longitude = jnp.arange(NLON, dtype=jnp.int32)
    phases = table_ids[:, None] * longitude[None, :] % NLON
    angles = phases.astype(jnp.float32) * (2.0 * math.pi / NLON)
    weight = jnp.where(table_ids == 0, 1.0, 2.0).astype(jnp.float32) / math.sqrt(2.0 * total_waves)
    cosine_part = (weight[:, None] * jnp.cos(angles)).astype(jnp.bfloat16)
    sine_part = (-weight[:, None] * jnp.sin(angles)).astype(jnp.bfloat16)
    table = jnp.concatenate([cosine_part, sine_part], axis=0)

    return synthesis([part for got in gathered for part in got], table)


def whole(coefficients, factors, wave_ids):
    return body(coefficients, factors, wave_ids)


MESH = pl.DeviceIdType.MESH
RING = 3


def exchange_kernel(
    unit,
    early,
    ids_ref,
    coef_ref,
    factor_ref,
    bands_ref,
    partial_ref,
    later_ref,
    coef_in,
    factor_in,
    factor_f32,
    factor,
    turn,
    mixed,
    ready,
    table,
    row_in,
    row_out,
    coef_sem,
    factor_sem,
    send_sem,
    recv_sem,
    band_send,
    band_recv,
    band_own,
    row_sem,
    out_sem,
    table_sem,
    free_sem,
):
    wave_pos, lev_pos = lax.axis_index("wave"), lax.axis_index("lev")
    lev_count = lax.axis_size("lev")
    rows, slots, channels = coef_ref.shape
    sections = factor_ref.shape[0]
    width = coef_in.shape[3]
    split = channels // width
    chunks = slots // unit * split
    band = rows // lev_count
    longitudes = table.shape[1]
    group = factor_in.shape[2]
    groups = rows // group
    jobs = sections * groups
    lane = 128

    def other(s):
        bit = 1 << s
        return jnp.where(wave_pos // bit % 2 == 0, wave_pos + bit, wave_pos - bit)

    def peer(d):
        return lax.rem(lev_pos + d, lev_count)

    barrier = pltpu.get_barrier_semaphore()
    for s in range(sections):
        pl.semaphore_signal(barrier, inc=1, device_id={"wave": other(s)}, device_id_type=MESH)
    for d in range(1, lev_count):
        pl.semaphore_signal(barrier, inc=1, device_id={"lev": peer(d)}, device_id_type=MESH)

    def place(c):
        low = pl.multiple_of(lax.div(c, split) * unit, unit)
        return pl.ds(low, unit), pl.ds(pl.multiple_of(lax.rem(c, split) * width, width), width)

    def coef_copy(c):
        k = lax.rem(c, 2)
        return pltpu.make_async_copy(coef_ref.at[(slice(None), *place(c))], coef_in.at[k], coef_sem.at[k])

    def factor_copy(j):
        k = lax.rem(j, 2)
        s, g = lax.div(j, groups), lax.rem(j, groups)
        return pltpu.make_async_copy(
            factor_ref.at[s, :, pl.ds(g * group, group)], factor_in.at[k], factor_sem.at[k]
        )

    for k in range(2):
        coef_copy(k).start()
        factor_copy(k).start()

    def slot(s, c):
        return s * RING + lax.rem(c, RING)

    def swap(s, c):
        k = slot(s, c)
        return pltpu.make_async_remote_copy(
            src_ref=mixed.at[k, :, pl.ds(0, rows), :],
            dst_ref=mixed.at[k, :, pl.ds(rows, rows), :],
            send_sem=send_sem.at[k],
            recv_sem=recv_sem.at[k],
            device_id={"wave": other(s)},
            device_id_type=MESH,
        )

    def band_copy(d, c, owner):
        k = lax.rem(c, RING)
        return pltpu.make_async_remote_copy(
            src_ref=ready.at[k, pl.ds(peer(d) * band, band)],
            dst_ref=bands_ref.at[(slice(None), owner, *place(c))],
            send_sem=band_send.at[k, d - 1],
            recv_sem=band_recv.at[c, d - 1],
            device_id={"lev": peer(d)},
            device_id_type=MESH,
        )

    def own_copy(c):
        k = lax.rem(c, RING)
        return pltpu.make_async_copy(
            ready.at[k, pl.ds(lev_pos * band, band)],
            bands_ref.at[(slice(None), lev_pos, *place(c))],
            band_own.at[k],
        )

    def release(s, c):
        @pl.when(c >= RING)
        def _():
            swap(s, c - RING).wait_send()

    def send(s, c):
        @pl.when(c >= RING)
        def _():
            pl.semaphore_wait(free_sem.at[s], 1)

        swap(s, c).start()

    degree = wave_pos * rows + lax.broadcasted_iota(jnp.int32, (rows, lane), 0)

    def begin(c):
        coef_copy(c).wait()
        for n, low in enumerate(range(0, width, lane)):
            part = coef_in[lax.rem(c, 2), :, :, pl.ds(low, lane)].astype(jnp.float32)
            turn[n] = part.reshape(rows * unit, lane)

        @pl.when(c + 2 < chunks)
        def _():
            coef_copy(c + 2).start()

        release(0, c)
        k = slot(0, c)
        for m in range(unit):
            live = degree >= ids_ref[pl.ds(lev_pos * slots + lax.div(c, split) * unit + m, 1), :]
            for n, low in enumerate(range(0, width, lane)):
                part = turn[n, pl.ds(m, rows, stride=unit), :]
                part = jnp.where(live, part, 0.0)
                mixed[k, m, pl.ds(0, rows), pl.ds(low, lane)] = part.astype(mixed.dtype)
        send(0, c)

    def prepare(s):
        def job(g, carry):
            j = s * groups + g
            factor_copy(j).wait()
            k = lax.rem(j, 2)
            for o in range(group):
                both = jnp.concatenate([factor_in[k, 0, o], factor_in[k, 1, o]], axis=0)
                rest = jnp.zeros((2 * lane - 2 * rows, slots), both.dtype)
                for n, part in enumerate((both[:lane], jnp.concatenate([both[lane:], rest], axis=0))):
                    factor_f32[n, pl.ds(o, slots, stride=group), :] = part.T.astype(jnp.float32)

            @pl.when(j + 2 < jobs)
            def _():
                factor_copy(j + 2).start()

            low = pl.multiple_of(g * group, group)
            for n in range(2):
                factor[pl.ds(s * slots, slots), pl.ds(low, group), pl.ds(n * lane, lane)] = (
                    factor_f32[n].astype(factor.dtype).reshape(slots, group, lane)
                )
            return carry

        lax.fori_loop(0, groups, job, 0)

    def mix(s, c):
        k = slot(s, c)
        swap(s, c).wait_recv()
        last = s == sections - 1
        if last:

            @pl.when(c >= RING)
            def _():
                for d in range(1, lev_count):
                    band_copy(d, c - RING, lev_pos).wait_send()
                own_copy(c - RING).wait()

        else:
            release(s + 1, c)
        for m in range(unit):
            total = jnp.dot(
                factor[s * slots + lax.div(c, split) * unit + m][:, : 2 * rows],
                mixed[k, m],
                preferred_element_type=jnp.float32,
            )
            if last:
                for n, low in enumerate(range(0, width, lane)):
                    turn[n, pl.ds(m, rows, stride=unit), :] = total[:, low : low + lane]
            else:
                mixed[slot(s + 1, c), m, pl.ds(0, rows), :] = total.astype(mixed.dtype)

        @pl.when(c < chunks - RING)
        def _():
            pl.semaphore_signal(free_sem.at[s], inc=1, device_id={"wave": other(s)}, device_id_type=MESH)

        if last:
            for n, low in enumerate(range(0, width, lane)):
                ready[lax.rem(c, RING), :, :, pl.ds(low, lane)] = (
                    turn[n].astype(ready.dtype).reshape(rows, unit, lane)
                )
            for d in (lev_count // 2, 1, lev_count - 1) if lev_count == 4 else range(1, lev_count):
                band_copy(d, c, lev_pos).start()
            own_copy(c).start()
        else:
            send(s + 1, c)

    def guarded(s, c):
        @pl.when((c >= 0) & (c < chunks))
        def _():
            mix(s, c)

    piece = math.gcd(early, slots)
    pieces = slots // piece
    ahead, behind = early * lev_count, (slots - early) * lev_count
    turnover = 2.0 * math.pi / longitudes

    def tabulate(i):
        owner, q = lax.div(i, pieces), lax.rem(i, pieces)
        ids = ids_ref[pl.ds(pl.multiple_of(owner * slots + q * piece, piece), piece), :]
        j = lax.broadcasted_iota(jnp.int32, ids.shape, 1)
        a = lax.rem(lax.rem(ids * lane, longitudes) * j, longitudes).astype(jnp.float32) * turnover
        b = lax.rem(ids * j, longitudes).astype(jnp.float32) * turnover
        weight = jnp.where(ids == 0, 1.0, 2.0) * (2.0 * slots * lev_count) ** -0.5
        cos_a, sin_a = weight * jnp.cos(a), weight * jnp.sin(a)
        cos_b, sin_b = jnp.cos(b), jnp.sin(b)
        first = q * piece < early
        low = jnp.where(first, owner * early + q * piece, 2 * ahead + (q * piece - early) * lev_count + owner * piece)
        high = low + jnp.where(first, ahead, behind)
        low, high = pl.multiple_of(low, piece), pl.multiple_of(high, piece)
        for n in range(longitudes // lane):
            ca, sa = cos_a[:, n : n + 1], sin_a[:, n : n + 1]
            columns = pl.ds(n * lane, lane)
            table[pl.ds(low, piece), columns] = (ca * cos_b - sa * sin_b).astype(table.dtype)
            table[pl.ds(high, piece), columns] = (-(sa * cos_b + ca * sin_b)).astype(table.dtype)

    later_copy = pltpu.make_async_copy(table.at[pl.ds(2 * ahead, 2 * behind)], later_ref, table_sem)
    tables = lev_count * pieces
    table_at = sections
    table_each = pl.cdiv(tables, early // unit * split - table_at)
    early_chunks = early // unit * split
    rows_at = early_chunks - 1 + RING + sections
    rows_each = pl.cdiv(band, chunks + sections - rows_at)

    def row_copy(r):
        k = lax.rem(r, 2)
        return pltpu.make_async_copy(bands_ref.at[r, :, pl.ds(0, early), :], row_in.at[k], row_sem.at[k])

    def out_copy(r):
        k = lax.rem(r, 2)
        return pltpu.make_async_copy(row_out.at[k], partial_ref.at[r], out_sem.at[k])

    def arrived(c, carry):
        for d in range(1, lev_count):
            band_copy(d, c, peer(lev_count - d)).wait_recv()
        return carry

    def synthesize(r):
        k = lax.rem(r, 2)
        row_copy(r).wait()

        @pl.when(r + 1 < band)
        def _():
            row_copy(r + 1).start()

        @pl.when(r >= 2)
        def _():
            out_copy(r - 2).wait()

        turned = row_in[k].reshape(ahead, channels).T
        spectrum = jnp.concatenate([turned[: channels // 2], turned[channels // 2 :]], axis=1)
        span = math.gcd(longitudes, 512)
        for j in range(0, longitudes, span):
            row_out[k, :, pl.ds(j, span)] = jnp.dot(
                spectrum, table[pl.ds(0, 2 * ahead), pl.ds(j, span)], preferred_element_type=jnp.float32
            ).astype(row_out.dtype)
        out_copy(r).start()

    pl.semaphore_wait(barrier, sections + lev_count - 1)

    def step(t, carry):
        guarded(0, t - 1)

        @pl.when(t < chunks)
        def _():
            begin(t)

        for s in range(1, sections - 1):
            guarded(s, t - 1 - s)

        @pl.when(t < sections)
        def _():
            prepare(t)

        guarded(sections - 1, t - sections)

        for n in range(table_each):
            i = (t - table_at) * table_each + n

            @pl.when((i >= 0) & (i < tables))
            def _():
                tabulate(i)

        @pl.when(t == rows_at)
        def _():
            later_copy.start()
            lax.fori_loop(0, early_chunks, arrived, 0)
            row_copy(0).start()

        for n in range(rows_each):
            r = (t - rows_at) * rows_each + n

            @pl.when((r >= 0) & (r < band))
            def _():
                synthesize(r)

        return carry

    lax.fori_loop(0, chunks + sections, step, 0)

    for c in range(chunks - RING, chunks):
        for s in range(sections):
            swap(s, jnp.int32(c)).wait_send()
        for d in range(1, lev_count):
            band_copy(d, jnp.int32(c), lev_pos).wait_send()
        own_copy(jnp.int32(c)).wait()

    lax.fori_loop(early_chunks, chunks, arrived, 0)
    for r in range(band - 2, band):
        out_copy(jnp.int32(r)).wait()
    later_copy.wait()


def exchange(ids, coefficients, factors, unit):
    lev_count = lax.axis_size("lev")
    rows, slots, channels = coefficients.shape
    sections = factors.shape[0]
    chunks = slots // unit * SPLIT
    width = channels // SPLIT
    band = rows // lev_count
    early = EARLY * unit
    kind = coefficients.dtype
    group = 16
    behind = (slots - early) * lev_count
    return pl.pallas_call(
        functools.partial(exchange_kernel, unit, early),
        out_shape=(
            jax.ShapeDtypeStruct((band, lev_count, slots, channels), kind),
            jax.ShapeDtypeStruct((band, channels // 2, NLON), kind),
            jax.ShapeDtypeStruct((2 * behind, NLON), kind),
        ),
        in_specs=[
            pl.BlockSpec(memory_space=pltpu.VMEM),
            pl.BlockSpec(memory_space=pltpu.HBM),
            pl.BlockSpec(memory_space=pltpu.HBM),
        ],
        out_specs=[pl.BlockSpec(memory_space=pltpu.HBM)] * 3,
        scratch_shapes=[
            pltpu.VMEM((2, rows, unit, width), kind),
            pltpu.VMEM((2, 2, group, rows, slots), kind),
            pltpu.VMEM((2, slots * group, 128), jnp.float32),
            pltpu.VMEM((sections * slots, rows, 256), kind),
            pltpu.VMEM((width // 128, rows * unit, 128), jnp.float32),
            pltpu.VMEM((sections * RING, unit, 2 * rows, width), kind),
            pltpu.VMEM((RING, rows, unit, width), kind),
            pltpu.VMEM((2 * lev_count * slots, NLON), kind),
            pltpu.VMEM((2, lev_count, early, channels), kind),
            pltpu.VMEM((2, channels // 2, NLON), kind),
            pltpu.SemaphoreType.DMA((2,)),
            pltpu.SemaphoreType.DMA((2,)),
            pltpu.SemaphoreType.DMA((sections * RING,)),
            pltpu.SemaphoreType.DMA((sections * RING,)),
            pltpu.SemaphoreType.DMA((RING, lev_count - 1)),
            pltpu.SemaphoreType.DMA((chunks, lev_count - 1)),
            pltpu.SemaphoreType.DMA((RING,)),
            pltpu.SemaphoreType.DMA((2,)),
            pltpu.SemaphoreType.DMA((2,)),
            pltpu.SemaphoreType.DMA,
            pltpu.SemaphoreType.REGULAR((sections,)),
        ],
        compiler_params=pltpu.CompilerParams(
            collective_id=0, has_side_effects=True, vmem_limit_bytes=60 << 20
        ),
    )(ids, coefficients, factors)


def finish_kernel(count, *refs):
    partial_ref, table_ref, out_ref = refs[count:]
    half = out_ref.shape[1]
    channels = refs[0].shape[3]
    wide = jnp.concatenate([ref[0].reshape(-1, channels) for ref in refs[:count]], axis=0)
    turned = wide.T
    spectrum = jnp.concatenate([turned[:half], turned[half:]], axis=1)
    span = math.gcd(out_ref.shape[2], 512)
    for j in range(0, out_ref.shape[2], span):
        total = jnp.dot(spectrum, table_ref[:, j : j + span], preferred_element_type=jnp.float32)
        total += partial_ref[0, :, j : j + span].astype(jnp.float32)
        out_ref[0, :, j : j + span] = total.astype(out_ref.dtype)


def finish(bands, partial, table, early):
    rows, owners, slots, channels = bands.shape
    piece = math.gcd(early, slots)
    starts = range(early // piece, slots // piece)
    whole_row = pl.BlockSpec((1, *partial.shape[1:]), lambda i: (i, 0, 0))
    return pl.pallas_call(
        functools.partial(finish_kernel, len(starts)),
        grid=(rows,),
        out_shape=jax.ShapeDtypeStruct(partial.shape, partial.dtype),
        in_specs=[pl.BlockSpec((1, owners, piece, channels), lambda i, n=n: (i, 0, n, 0)) for n in starts]
        + [whole_row, pl.BlockSpec(table.shape, lambda i: (0, 0), pipeline_mode=pl.Buffered(1))],
        out_specs=whole_row,
        cost_estimate=pl.CostEstimate(
            flops=2 * partial.size * table.shape[0],
            bytes_accessed=2 * (2 * partial.size + table.size),
            transcendentals=0,
        ),
    )(*[bands] * len(starts), partial, table)


def unit_of(rows, slots):
    return UNIT if rows % 16 == 0 and 128 <= 2 * rows <= 256 and slots % UNIT == 0 and slots // UNIT > EARLY + RING else 0


def staged(coefficients, factors, wave_ids):
    rows, slots, _ = coefficients.shape
    unit = unit_of(rows, slots)
    ids = jnp.broadcast_to(wave_ids[:, None], (wave_ids.shape[0], 128))
    bands, partial, table = exchange(ids, coefficients, factors, unit)
    return finish(bands, partial, table, EARLY * unit)


def solution(mesh):
    in_specs = (P("wave", "lev", None), P(None, None, "wave", None, "lev"), P())
    out_specs = P(("wave", "lev"), None, None)

    def mapped(step):
        return jax.shard_map(step, mesh=mesh, in_specs=in_specs, out_specs=out_specs, check_vma=False)

    def run(coefficients, factors, wave_ids):
        lev_count = mesh.shape["lev"]
        slots = coefficients.shape[1] // lev_count
        if unit_of(factors.shape[3], slots):
            return mapped(staged)(coefficients, factors, wave_ids)
        return mapped(whole)(coefficients, factors, wave_ids)

    return run
```

```python
import functools
import math

import jax
import jax.numpy as jnp
from jax import lax
from jax.experimental import pallas as pl
from jax.experimental.pallas import tpu as pltpu
from jax.sharding import PartitionSpec as P


NLON = 2560
UNIT = 8
SPLIT = 2
EARLY = 16
TALL = 2


def swapped(block, axis, apart):
    count = lax.axis_size(axis)
    route = []
    for low in range(count):
        high = low | 1 << apart
        if high != low and high < count:
            route += [(low, high), (high, low)]
    return lax.ppermute(block, axis, route)


def combine_kernel(count, factor_ref, own_ref, partner_ref, *refs):
    out_ref = refs[-1]
    for m in range(count):
        total = jnp.dot(factor_ref[0, m], own_ref[m], preferred_element_type=jnp.float32)
        total += jnp.dot(factor_ref[1, m], partner_ref[m], preferred_element_type=jnp.float32)
        out_ref[m] = total.astype(out_ref.dtype)


def combine(factor, own, partner, start, after):
    slots, rows, channels = own.shape
    step = math.gcd(slots, 8)
    block = pl.BlockSpec((step, rows, channels), lambda i: (i, 0, 0))
    return pl.pallas_call(
        functools.partial(combine_kernel, step),
        grid=(slots // step,),
        out_shape=jax.ShapeDtypeStruct(own.shape, own.dtype),
        in_specs=[
            pl.BlockSpec((2, step, rows, rows), lambda i: (0, start // step + i, 0, 0)),
            block,
            block,
        ]
        + [pl.BlockSpec(memory_space=pl.ANY)] * len(after),
        out_specs=block,
        cost_estimate=pl.CostEstimate(
            flops=4 * slots * rows * rows * channels,
            bytes_accessed=2 * (3 * own.size + 2 * slots * rows * rows),
            transcendentals=0,
        ),
    )(factor, own, partner, *after)


def synthesis_kernel(count, *refs):
    table_ref, out_ref = refs[count], refs[count + 1]
    half = out_ref.shape[1]
    wide = jnp.concatenate([ref[0] for ref in refs[:count]], axis=0)
    turned = wide.T
    spectrum = jnp.concatenate([turned[:half], turned[half:]], axis=1)
    span = math.gcd(out_ref.shape[2], 512)
    for j in range(0, out_ref.shape[2], span):
        out_ref[0, :, j : j + span] = jnp.dot(
            spectrum, table_ref[:, j : j + span], preferred_element_type=jnp.float32
        ).astype(out_ref.dtype)


def synthesis(parts, table):
    rows, _, channels = parts[0].shape
    depth, longitudes = table.shape
    return pl.pallas_call(
        functools.partial(synthesis_kernel, len(parts)),
        grid=(rows,),
        out_shape=jax.ShapeDtypeStruct((rows, channels // 2, longitudes), parts[0].dtype),
        in_specs=[pl.BlockSpec((1, p.shape[1], channels), lambda i: (i, 0, 0)) for p in parts]
        + [pl.BlockSpec((depth, longitudes), lambda i: (0, 0), pipeline_mode=pl.Buffered(1))],
        out_specs=pl.BlockSpec((1, channels // 2, longitudes), lambda i: (i, 0, 0)),
        cost_estimate=pl.CostEstimate(
            flops=rows * channels * depth * longitudes,
            bytes_accessed=rows * channels * (depth + longitudes) + 2 * table.size,
            transcendentals=0,
        ),
    )(*parts, table)


def cuts_of(slots):
    unit = math.gcd(slots, 16)
    edges = [0]
    while edges[-1] < slots:
        left = slots - edges[-1]
        edges.append(edges[-1] + (unit if edges[-1] == 0 or left <= 2 * unit else 2 * unit))
    return list(zip(edges[:-1], edges[1:]))


def mixes(pieces, sections):
    return [
        (t - s - (s > 0), s)
        for t in range(pieces + sections + 1)
        for s in range(sections)
        if 0 <= t - s - (s > 0) < pieces
    ]


def body(coefficients, factors, wave_ids):
    wave_count = lax.axis_size("wave")
    lev_count = lax.axis_size("lev")
    sections = wave_count.bit_length() - 1
    rows, slots, _ = coefficients.shape
    total_waves = wave_ids.shape[0]
    wave_pos = lax.axis_index("wave")
    lev_pos = lax.axis_index("lev")
    cuts = cuts_of(slots)
    pieces = len(cuts)
    band = rows // lev_count
    ids = [
        lax.dynamic_slice_in_dim(wave_ids, (lev_pos - d) % lev_count * slots, slots, 0)
        for d in range(lev_count)
    ]
    degree = wave_pos * rows + jnp.arange(rows, dtype=jnp.int32)
    factor = [factors[s].transpose(0, 3, 1, 2) for s in range(sections)]

    current = [None] * pieces
    gathered = [None] * pieces

    def start(c):
        low, high = cuts[c]
        live = (degree[:, None] >= ids[0][low:high][None, :])[:, :, None]
        block = coefficients[:, low:high, :]
        block = jnp.where(live, block, jnp.zeros((), block.dtype))
        return block.transpose(1, 0, 2)

    def spread(c):
        ready = current[c].transpose(1, 0, 2)
        got = [lax.dynamic_slice_in_dim(ready, lev_pos * band, band, 0)]
        for d in range(1, lev_count):
            part = lax.dynamic_slice_in_dim(ready, (lev_pos + d) % lev_count * band, band, 0)
            route = [(k, (k + d) % lev_count) for k in range(lev_count)]
            got.append(lax.ppermute(part, "lev", route))
        gathered[c] = got

    for c in range(pieces):
        current[c] = start(c)
    after = []
    for c, s in mixes(pieces, sections):
        partner = swapped(current[c], "wave", s)
        current[c] = combine(factor[s], current[c], partner, cuts[c][0], after)
        after = [current[c]]
        if s == sections - 1:
            spread(c)

    table_ids = jnp.concatenate([ids[d][low:high] for low, high in cuts for d in range(lev_count)])
    longitude = jnp.arange(NLON, dtype=jnp.int32)
    phases = table_ids[:, None] * longitude[None, :] % NLON
    angles = phases.astype(jnp.float32) * (2.0 * math.pi / NLON)
    weight = jnp.where(table_ids == 0, 1.0, 2.0).astype(jnp.float32) / math.sqrt(2.0 * total_waves)
    cosine_part = (weight[:, None] * jnp.cos(angles)).astype(jnp.bfloat16)
    sine_part = (-weight[:, None] * jnp.sin(angles)).astype(jnp.bfloat16)
    table = jnp.concatenate([cosine_part, sine_part], axis=0)

    return synthesis([part for got in gathered for part in got], table)


def whole(coefficients, factors, wave_ids):
    return body(coefficients, factors, wave_ids)


MESH = pl.DeviceIdType.MESH
RING = 3


def exchange_kernel(
    unit,
    early,
    ids_ref,
    coef_ref,
    factor_ref,
    bands_ref,
    partial_ref,
    later_ref,
    coef_in,
    factor_in,
    factor_f32,
    factor,
    turn,
    mixed,
    ready,
    table,
    row_in,
    row_out,
    coef_sem,
    factor_sem,
    send_sem,
    recv_sem,
    band_send,
    band_recv,
    band_own,
    row_sem,
    out_sem,
    table_sem,
    free_sem,
):
    wave_pos, lev_pos = lax.axis_index("wave"), lax.axis_index("lev")
    lev_count = lax.axis_size("lev")
    rows, slots, channels = coef_ref.shape
    sections = factor_ref.shape[0]
    width = coef_in.shape[3]
    split = channels // width
    chunks = slots // unit * split
    band = rows // lev_count
    longitudes = table.shape[1]
    group = factor_in.shape[2]
    groups = rows // group
    jobs = sections * groups
    lane = 128
    front = min(slots, lane)

    def other(s):
        bit = 1 << s
        return jnp.where(wave_pos // bit % 2 == 0, wave_pos + bit, wave_pos - bit)

    def peer(d):
        return lax.rem(lev_pos + d, lev_count)

    barrier = pltpu.get_barrier_semaphore()
    for s in range(sections):
        pl.semaphore_signal(barrier, inc=1, device_id={"wave": other(s)}, device_id_type=MESH)
    for d in range(1, lev_count):
        pl.semaphore_signal(barrier, inc=1, device_id={"lev": peer(d)}, device_id_type=MESH)

    def place(c):
        low = pl.multiple_of(lax.div(c, split) * unit, unit)
        return pl.ds(low, unit), pl.ds(pl.multiple_of(lax.rem(c, split) * width, width), width)

    def coef_copy(c):
        k = lax.rem(c, 2)
        return pltpu.make_async_copy(coef_ref.at[(slice(None), *place(c))], coef_in.at[k], coef_sem.at[k])

    def factor_copy(j):
        k = lax.rem(j, 2)
        s, g = lax.div(lax.rem(j, jobs), groups), lax.rem(j, groups)
        return pltpu.make_async_copy(
            factor_ref.at[s, :, pl.ds(g * group, group)], factor_in.at[k], factor_sem.at[k]
        )

    for k in range(2):
        coef_copy(k).start()
        factor_copy(k).start()

    def slot(s, c):
        return s * RING + lax.rem(c, RING)

    def swap(s, c):
        k = slot(s, c)
        return pltpu.make_async_remote_copy(
            src_ref=mixed.at[k, :, pl.ds(0, rows), :],
            dst_ref=mixed.at[k, :, pl.ds(rows, rows), :],
            send_sem=send_sem.at[k],
            recv_sem=recv_sem.at[k],
            device_id={"wave": other(s)},
            device_id_type=MESH,
        )

    def band_copy(d, c, owner):
        k = lax.rem(c, RING)
        return pltpu.make_async_remote_copy(
            src_ref=ready.at[k, pl.ds(peer(d) * band, band)],
            dst_ref=bands_ref.at[(slice(None), owner, *place(c))],
            send_sem=band_send.at[k, d - 1],
            recv_sem=band_recv.at[c, d - 1],
            device_id={"lev": peer(d)},
            device_id_type=MESH,
        )

    def own_copy(c):
        k = lax.rem(c, RING)
        return pltpu.make_async_copy(
            ready.at[k, pl.ds(lev_pos * band, band)],
            bands_ref.at[(slice(None), lev_pos, *place(c))],
            band_own.at[k],
        )

    def release(s, c):
        @pl.when(c >= RING)
        def _():
            swap(s, c - RING).wait_send()

    def send(s, c):
        @pl.when(c >= RING)
        def _():
            pl.semaphore_wait(free_sem.at[s], 1)

        swap(s, c).start()

    degree = wave_pos * rows + lax.broadcasted_iota(jnp.int32, (rows, lane), 0)

    def begin(c):
        coef_copy(c).wait()
        for n, low in enumerate(range(0, width, lane)):
            part = coef_in[lax.rem(c, 2), :, :, pl.ds(low, lane)].astype(jnp.float32)
            turn[n] = part.reshape(rows * unit, lane)

        @pl.when(c + 2 < chunks)
        def _():
            coef_copy(c + 2).start()

        release(0, c)
        k = slot(0, c)
        for m in range(unit):
            live = degree >= ids_ref[pl.ds(lev_pos * slots + lax.div(c, split) * unit + m, 1), :]
            for n, low in enumerate(range(0, width, lane)):
                part = turn[n, pl.ds(m, rows, stride=unit), :]
                part = jnp.where(live, part, 0.0)
                mixed[k, m, pl.ds(0, rows), pl.ds(low, lane)] = part.astype(mixed.dtype)
        send(0, c)

    def rearrange(j, low, count):
        s, g = lax.div(lax.rem(j, jobs), groups), lax.rem(j, groups)
        k = lax.rem(j, 2)
        factor_copy(j).wait()
        for o in range(group):
            both = jnp.concatenate(
                [factor_in[k, q, o, :, pl.ds(low, count)] for q in range(2)]
                + [jnp.zeros((2 * lane - 2 * rows, count), factor_in.dtype)],
                axis=0,
            )
            for n in range(2):
                factor_f32[n, pl.ds(o, count, stride=group), :] = (
                    both[n * lane : (n + 1) * lane].T.astype(jnp.float32)
                )

        @pl.when(j + 2 < 2 * jobs)
        def _():
            factor_copy(j + 2).start()

        row = pl.multiple_of(g * group, group)
        for n in range(2):
            factor[pl.ds(s * slots + low, count), pl.ds(row, group), pl.ds(n * lane, lane)] = (
                factor_f32[n, pl.ds(0, count * group), :].astype(factor.dtype).reshape(count, group, lane)
            )

    def prepare(s):
        def job(g, carry):
            rearrange(s * groups + g, 0, front)
            return carry

        lax.fori_loop(0, groups, job, 0)

    def mix(s, c):
        k = slot(s, c)
        swap(s, c).wait_recv()
        last = s == sections - 1
        if last:

            @pl.when(c >= RING)
            def _():
                for d in range(1, lev_count):
                    band_copy(d, c - RING, lev_pos).wait_send()
                own_copy(c - RING).wait()

        else:
            release(s + 1, c)
        for m in range(unit):
            total = jnp.dot(
                factor[s * slots + lax.div(c, split) * unit + m][:, : 2 * rows],
                mixed[k, m],
                preferred_element_type=jnp.float32,
            )
            if last:
                for n, low in enumerate(range(0, width, lane)):
                    turn[n, pl.ds(m, rows, stride=unit), :] = total[:, low : low + lane]
            else:
                mixed[slot(s + 1, c), m, pl.ds(0, rows), :] = total.astype(mixed.dtype)

        @pl.when(c < chunks - RING)
        def _():
            pl.semaphore_signal(free_sem.at[s], inc=1, device_id={"wave": other(s)}, device_id_type=MESH)

        if last:
            for n, low in enumerate(range(0, width, lane)):
                ready[lax.rem(c, RING), :, :, pl.ds(low, lane)] = (
                    turn[n].astype(ready.dtype).reshape(rows, unit, lane)
                )
            for d in (lev_count // 2, 1, lev_count - 1) if lev_count == 4 else range(1, lev_count):
                band_copy(d, c, lev_pos).start()
            own_copy(c).start()
        else:
            send(s + 1, c)

    def guarded(s, c):
        @pl.when((c >= 0) & (c < chunks))
        def _():
            mix(s, c)

    piece = math.gcd(early, slots)
    pieces = slots // piece
    ahead, behind = early * lev_count, (slots - early) * lev_count
    turnover = 2.0 * math.pi / longitudes

    def tabulate(i):
        owner, q = lax.div(i, pieces), lax.rem(i, pieces)
        ids = ids_ref[pl.ds(pl.multiple_of(owner * slots + q * piece, piece), piece), :]
        j = lax.broadcasted_iota(jnp.int32, ids.shape, 1)
        a = lax.rem(lax.rem(ids * lane, longitudes) * j, longitudes).astype(jnp.float32) * turnover
        b = lax.rem(ids * j, longitudes).astype(jnp.float32) * turnover
        weight = jnp.where(ids == 0, 1.0, 2.0) * (2.0 * slots * lev_count) ** -0.5
        cos_a, sin_a = weight * jnp.cos(a), weight * jnp.sin(a)
        cos_b, sin_b = jnp.cos(b), jnp.sin(b)
        first = q * piece < early
        low = jnp.where(first, owner * early + q * piece, 2 * ahead + (q * piece - early) * lev_count + owner * piece)
        high = low + jnp.where(first, ahead, behind)
        low, high = pl.multiple_of(low, piece), pl.multiple_of(high, piece)
        for n in range(longitudes // lane):
            ca, sa = cos_a[:, n : n + 1], sin_a[:, n : n + 1]
            columns = pl.ds(n * lane, lane)
            table[pl.ds(low, piece), columns] = (ca * cos_b - sa * sin_b).astype(table.dtype)
            table[pl.ds(high, piece), columns] = (-(sa * cos_b + ca * sin_b)).astype(table.dtype)

    later_copy = pltpu.make_async_copy(table.at[pl.ds(2 * ahead, 2 * behind)], later_ref, table_sem)
    tables = lev_count * pieces
    table_at = sections
    table_each = pl.cdiv(tables, early // unit * split - table_at)
    early_chunks = early // unit * split
    rows_at = early_chunks - 1 + RING + sections
    rows_each = pl.cdiv(band, chunks + sections - rows_at)

    def row_copy(r):
        k = lax.rem(r, 2)
        return pltpu.make_async_copy(bands_ref.at[r, :, pl.ds(0, early), :], row_in.at[k], row_sem.at[k])

    def out_copy(r):
        k = lax.rem(r, 2)
        return pltpu.make_async_copy(row_out.at[k], partial_ref.at[r], out_sem.at[k])

    def arrived(c, carry):
        for d in range(1, lev_count):
            band_copy(d, c, peer(lev_count - d)).wait_recv()
        return carry

    def synthesize(r):
        k = lax.rem(r, 2)
        row_copy(r).wait()

        @pl.when(r + 1 < band)
        def _():
            row_copy(r + 1).start()

        @pl.when(r >= 2)
        def _():
            out_copy(r - 2).wait()

        turned = row_in[k].reshape(ahead, channels).T
        spectrum = jnp.concatenate([turned[: channels // 2], turned[channels // 2 :]], axis=1)
        span = math.gcd(longitudes, 512)
        for j in range(0, longitudes, span):
            row_out[k, :, pl.ds(j, span)] = jnp.dot(
                spectrum, table[pl.ds(0, 2 * ahead), pl.ds(j, span)], preferred_element_type=jnp.float32
            ).astype(row_out.dtype)
        out_copy(r).start()

    pl.semaphore_wait(barrier, sections + lev_count - 1)

    def step(t, carry):
        guarded(0, t - 1)

        @pl.when(t < chunks)
        def _():
            begin(t)

        for s in range(1, sections - 1):
            guarded(s, t - 1 - s)

        @pl.when(t < sections)
        def _():
            prepare(t)

        guarded(sections - 1, t - sections)

        @pl.when((t > sections) & (t <= sections + jobs))
        def _():
            rearrange(jobs + t - sections - 1, front, slots - front)

        for n in range(table_each):
            i = (t - table_at) * table_each + n

            @pl.when((i >= 0) & (i < tables))
            def _():
                tabulate(i)

        @pl.when(t == rows_at)
        def _():
            later_copy.start()
            lax.fori_loop(0, early_chunks, arrived, 0)
            row_copy(0).start()

        for n in range(rows_each):
            r = (t - rows_at) * rows_each + n

            @pl.when((r >= 0) & (r < band))
            def _():
                synthesize(r)

        return carry

    lax.fori_loop(0, chunks + sections, step, 0)

    for c in range(chunks - RING, chunks):
        for s in range(sections):
            swap(s, jnp.int32(c)).wait_send()
        for d in range(1, lev_count):
            band_copy(d, jnp.int32(c), lev_pos).wait_send()
        own_copy(jnp.int32(c)).wait()

    lax.fori_loop(early_chunks, chunks, arrived, 0)
    for r in range(band - 2, band):
        out_copy(jnp.int32(r)).wait()
    later_copy.wait()


def exchange(ids, coefficients, factors, unit):
    lev_count = lax.axis_size("lev")
    rows, slots, channels = coefficients.shape
    sections = factors.shape[0]
    chunks = slots // unit * SPLIT
    width = channels // SPLIT
    band = rows // lev_count
    early = EARLY * unit
    kind = coefficients.dtype
    group = 16
    behind = (slots - early) * lev_count
    return pl.pallas_call(
        functools.partial(exchange_kernel, unit, early),
        out_shape=(
            jax.ShapeDtypeStruct((band, lev_count, slots, channels), kind),
            jax.ShapeDtypeStruct((band, channels // 2, NLON), kind),
            jax.ShapeDtypeStruct((2 * behind, NLON), kind),
        ),
        in_specs=[
            pl.BlockSpec(memory_space=pltpu.VMEM),
            pl.BlockSpec(memory_space=pltpu.HBM),
            pl.BlockSpec(memory_space=pltpu.HBM),
        ],
        out_specs=[pl.BlockSpec(memory_space=pltpu.HBM)] * 3,
        scratch_shapes=[
            pltpu.VMEM((2, rows, unit, width), kind),
            pltpu.VMEM((2, 2, group, rows, slots), kind),
            pltpu.VMEM((2, 128 * group, 128), jnp.float32),
            pltpu.VMEM((sections * slots, rows, 256), kind),
            pltpu.VMEM((width // 128, rows * unit, 128), jnp.float32),
            pltpu.VMEM((sections * RING, unit, 2 * rows, width), kind),
            pltpu.VMEM((RING, rows, unit, width), kind),
            pltpu.VMEM((2 * lev_count * slots, NLON), kind),
            pltpu.VMEM((2, lev_count, early, channels), kind),
            pltpu.VMEM((2, channels // 2, NLON), kind),
            pltpu.SemaphoreType.DMA((2,)),
            pltpu.SemaphoreType.DMA((2,)),
            pltpu.SemaphoreType.DMA((sections * RING,)),
            pltpu.SemaphoreType.DMA((sections * RING,)),
            pltpu.SemaphoreType.DMA((RING, lev_count - 1)),
            pltpu.SemaphoreType.DMA((chunks, lev_count - 1)),
            pltpu.SemaphoreType.DMA((RING,)),
            pltpu.SemaphoreType.DMA((2,)),
            pltpu.SemaphoreType.DMA((2,)),
            pltpu.SemaphoreType.DMA,
            pltpu.SemaphoreType.REGULAR((sections,)),
        ],
        compiler_params=pltpu.CompilerParams(
            collective_id=0, has_side_effects=True, vmem_limit_bytes=60 << 20
        ),
    )(ids, coefficients, factors)


def finish_kernel(count, *refs):
    partial_ref, table_ref, out_ref = refs[count:]
    tall, half, longitudes = out_ref.shape
    channels = refs[0].shape[3]
    lines = []
    for r in range(tall):
        wide = jnp.concatenate([ref[r].reshape(-1, channels) for ref in refs[:count]], axis=0)
        turned = wide.T
        lines.append(jnp.concatenate([turned[:half], turned[half:]], axis=1))
    spectrum = jnp.concatenate(lines, axis=0)
    span = math.gcd(longitudes, 512)
    for j in range(0, longitudes, span):
        total = jnp.dot(spectrum, table_ref[:, j : j + span], preferred_element_type=jnp.float32)
        for r in range(tall):
            own = total[r * half : (r + 1) * half] + partial_ref[r, :, j : j + span].astype(jnp.float32)
            out_ref[r, :, j : j + span] = own.astype(out_ref.dtype)


def finish(bands, partial, table, early):
    rows, owners, slots, channels = bands.shape
    tall = math.gcd(rows, TALL)
    piece = math.gcd(early, slots)
    starts = range(early // piece, slots // piece)
    whole_row = pl.BlockSpec((tall, *partial.shape[1:]), lambda i: (i, 0, 0))
    return pl.pallas_call(
        functools.partial(finish_kernel, len(starts)),
        grid=(rows // tall,),
        out_shape=jax.ShapeDtypeStruct(partial.shape, partial.dtype),
        in_specs=[pl.BlockSpec((tall, owners, piece, channels), lambda i, n=n: (i, 0, n, 0)) for n in starts]
        + [whole_row, pl.BlockSpec(table.shape, lambda i: (0, 0), pipeline_mode=pl.Buffered(1))],
        out_specs=whole_row,
        cost_estimate=pl.CostEstimate(
            flops=2 * partial.size * table.shape[0],
            bytes_accessed=2 * (2 * partial.size + table.size),
            transcendentals=0,
        ),
    )(*[bands] * len(starts), partial, table)


def unit_of(rows, slots):
    return UNIT if rows % 16 == 0 and 128 <= 2 * rows <= 256 and 128 < slots <= 256 and slots % UNIT == 0 and slots // UNIT > EARLY + RING else 0


def staged(coefficients, factors, wave_ids):
    rows, slots, _ = coefficients.shape
    unit = unit_of(rows, slots)
    ids = jnp.broadcast_to(wave_ids[:, None], (wave_ids.shape[0], 128))
    bands, partial, table = exchange(ids, coefficients, factors, unit)
    return finish(bands, partial, table, EARLY * unit)


def solution(mesh):
    in_specs = (P("wave", "lev", None), P(None, None, "wave", None, "lev"), P())
    out_specs = P(("wave", "lev"), None, None)

    def mapped(step):
        return jax.shard_map(step, mesh=mesh, in_specs=in_specs, out_specs=out_specs, check_vma=False)

    def run(coefficients, factors, wave_ids):
        lev_count = mesh.shape["lev"]
        slots = coefficients.shape[1] // lev_count
        if unit_of(factors.shape[3], slots):
            return mapped(staged)(coefficients, factors, wave_ids)
        return mapped(whole)(coefficients, factors, wave_ids)

    return run
```

```python
import functools
import math

import jax
import jax.numpy as jnp
from jax import lax
from jax.experimental import pallas as pl
from jax.experimental.pallas import tpu as pltpu
from jax.sharding import PartitionSpec as P


NLON = 2560
UNIT = 8
SPLIT = 2
EARLY = 16
TALL = 4


def swapped(block, axis, apart):
    count = lax.axis_size(axis)
    route = []
    for low in range(count):
        high = low | 1 << apart
        if high != low and high < count:
            route += [(low, high), (high, low)]
    return lax.ppermute(block, axis, route)


def combine_kernel(count, factor_ref, own_ref, partner_ref, *refs):
    out_ref = refs[-1]
    for m in range(count):
        total = jnp.dot(factor_ref[0, m], own_ref[m], preferred_element_type=jnp.float32)
        total += jnp.dot(factor_ref[1, m], partner_ref[m], preferred_element_type=jnp.float32)
        out_ref[m] = total.astype(out_ref.dtype)


def combine(factor, own, partner, start, after):
    slots, rows, channels = own.shape
    step = math.gcd(slots, 8)
    block = pl.BlockSpec((step, rows, channels), lambda i: (i, 0, 0))
    return pl.pallas_call(
        functools.partial(combine_kernel, step),
        grid=(slots // step,),
        out_shape=jax.ShapeDtypeStruct(own.shape, own.dtype),
        in_specs=[
            pl.BlockSpec((2, step, rows, rows), lambda i: (0, start // step + i, 0, 0)),
            block,
            block,
        ]
        + [pl.BlockSpec(memory_space=pl.ANY)] * len(after),
        out_specs=block,
        cost_estimate=pl.CostEstimate(
            flops=4 * slots * rows * rows * channels,
            bytes_accessed=2 * (3 * own.size + 2 * slots * rows * rows),
            transcendentals=0,
        ),
    )(factor, own, partner, *after)


def synthesis_kernel(count, *refs):
    table_ref, out_ref = refs[count], refs[count + 1]
    half = out_ref.shape[1]
    wide = jnp.concatenate([ref[0] for ref in refs[:count]], axis=0)
    turned = wide.T
    spectrum = jnp.concatenate([turned[:half], turned[half:]], axis=1)
    span = math.gcd(out_ref.shape[2], 512)
    for j in range(0, out_ref.shape[2], span):
        out_ref[0, :, j : j + span] = jnp.dot(
            spectrum, table_ref[:, j : j + span], preferred_element_type=jnp.float32
        ).astype(out_ref.dtype)


def synthesis(parts, table):
    rows, _, channels = parts[0].shape
    depth, longitudes = table.shape
    return pl.pallas_call(
        functools.partial(synthesis_kernel, len(parts)),
        grid=(rows,),
        out_shape=jax.ShapeDtypeStruct((rows, channels // 2, longitudes), parts[0].dtype),
        in_specs=[pl.BlockSpec((1, p.shape[1], channels), lambda i: (i, 0, 0)) for p in parts]
        + [pl.BlockSpec((depth, longitudes), lambda i: (0, 0), pipeline_mode=pl.Buffered(1))],
        out_specs=pl.BlockSpec((1, channels // 2, longitudes), lambda i: (i, 0, 0)),
        cost_estimate=pl.CostEstimate(
            flops=rows * channels * depth * longitudes,
            bytes_accessed=rows * channels * (depth + longitudes) + 2 * table.size,
            transcendentals=0,
        ),
    )(*parts, table)


def cuts_of(slots):
    unit = math.gcd(slots, 16)
    edges = [0]
    while edges[-1] < slots:
        left = slots - edges[-1]
        edges.append(edges[-1] + (unit if edges[-1] == 0 or left <= 2 * unit else 2 * unit))
    return list(zip(edges[:-1], edges[1:]))


def mixes(pieces, sections):
    return [
        (t - s - (s > 0), s)
        for t in range(pieces + sections + 1)
        for s in range(sections)
        if 0 <= t - s - (s > 0) < pieces
    ]


def body(coefficients, factors, wave_ids):
    wave_count = lax.axis_size("wave")
    lev_count = lax.axis_size("lev")
    sections = wave_count.bit_length() - 1
    rows, slots, _ = coefficients.shape
    total_waves = wave_ids.shape[0]
    wave_pos = lax.axis_index("wave")
    lev_pos = lax.axis_index("lev")
    cuts = cuts_of(slots)
    pieces = len(cuts)
    band = rows // lev_count
    ids = [
        lax.dynamic_slice_in_dim(wave_ids, (lev_pos - d) % lev_count * slots, slots, 0)
        for d in range(lev_count)
    ]
    degree = wave_pos * rows + jnp.arange(rows, dtype=jnp.int32)
    factor = [factors[s].transpose(0, 3, 1, 2) for s in range(sections)]

    current = [None] * pieces
    gathered = [None] * pieces

    def start(c):
        low, high = cuts[c]
        live = (degree[:, None] >= ids[0][low:high][None, :])[:, :, None]
        block = coefficients[:, low:high, :]
        block = jnp.where(live, block, jnp.zeros((), block.dtype))
        return block.transpose(1, 0, 2)

    def spread(c):
        ready = current[c].transpose(1, 0, 2)
        got = [lax.dynamic_slice_in_dim(ready, lev_pos * band, band, 0)]
        for d in range(1, lev_count):
            part = lax.dynamic_slice_in_dim(ready, (lev_pos + d) % lev_count * band, band, 0)
            route = [(k, (k + d) % lev_count) for k in range(lev_count)]
            got.append(lax.ppermute(part, "lev", route))
        gathered[c] = got

    for c in range(pieces):
        current[c] = start(c)
    after = []
    for c, s in mixes(pieces, sections):
        partner = swapped(current[c], "wave", s)
        current[c] = combine(factor[s], current[c], partner, cuts[c][0], after)
        after = [current[c]]
        if s == sections - 1:
            spread(c)

    table_ids = jnp.concatenate([ids[d][low:high] for low, high in cuts for d in range(lev_count)])
    longitude = jnp.arange(NLON, dtype=jnp.int32)
    phases = table_ids[:, None] * longitude[None, :] % NLON
    angles = phases.astype(jnp.float32) * (2.0 * math.pi / NLON)
    weight = jnp.where(table_ids == 0, 1.0, 2.0).astype(jnp.float32) / math.sqrt(2.0 * total_waves)
    cosine_part = (weight[:, None] * jnp.cos(angles)).astype(jnp.bfloat16)
    sine_part = (-weight[:, None] * jnp.sin(angles)).astype(jnp.bfloat16)
    table = jnp.concatenate([cosine_part, sine_part], axis=0)

    return synthesis([part for got in gathered for part in got], table)


def whole(coefficients, factors, wave_ids):
    return body(coefficients, factors, wave_ids)


MESH = pl.DeviceIdType.MESH
RING = 3


def exchange_kernel(
    unit,
    early,
    ids_ref,
    coef_ref,
    factor_ref,
    bands_ref,
    partial_ref,
    later_ref,
    coef_in,
    factor_in,
    factor_f32,
    factor,
    turn,
    mixed,
    ready,
    table,
    row_in,
    row_out,
    coef_sem,
    factor_sem,
    send_sem,
    recv_sem,
    band_send,
    band_recv,
    band_own,
    row_sem,
    out_sem,
    table_sem,
    free_sem,
):
    wave_pos, lev_pos = lax.axis_index("wave"), lax.axis_index("lev")
    lev_count = lax.axis_size("lev")
    rows, slots, channels = coef_ref.shape
    sections = factor_ref.shape[0]
    width = coef_in.shape[3]
    split = channels // width
    chunks = slots // unit * split
    band = rows // lev_count
    longitudes = table.shape[1]
    group = factor_in.shape[2]
    groups = rows // group
    jobs = sections * groups
    lane = 128
    front = min(slots, lane)

    def other(s):
        bit = 1 << s
        return jnp.where(wave_pos // bit % 2 == 0, wave_pos + bit, wave_pos - bit)

    def peer(d):
        return lax.rem(lev_pos + d, lev_count)

    barrier = pltpu.get_barrier_semaphore()
    for s in range(sections):
        pl.semaphore_signal(barrier, inc=1, device_id={"wave": other(s)}, device_id_type=MESH)
    for d in range(1, lev_count):
        pl.semaphore_signal(barrier, inc=1, device_id={"lev": peer(d)}, device_id_type=MESH)

    def place(c):
        low = pl.multiple_of(lax.div(c, split) * unit, unit)
        return pl.ds(low, unit), pl.ds(pl.multiple_of(lax.rem(c, split) * width, width), width)

    def coef_copy(c):
        k = lax.rem(c, 2)
        return pltpu.make_async_copy(coef_ref.at[(slice(None), *place(c))], coef_in.at[k], coef_sem.at[k])

    def factor_copy(j):
        k = lax.rem(j, 2)
        s, g = lax.div(lax.rem(j, jobs), groups), lax.rem(j, groups)
        return pltpu.make_async_copy(
            factor_ref.at[s, :, pl.ds(g * group, group)], factor_in.at[k], factor_sem.at[k]
        )

    for k in range(2):
        coef_copy(k).start()
        factor_copy(k).start()

    def slot(s, c):
        return s * RING + lax.rem(c, RING)

    def swap(s, c):
        k = slot(s, c)
        return pltpu.make_async_remote_copy(
            src_ref=mixed.at[k, :, pl.ds(0, rows), :],
            dst_ref=mixed.at[k, :, pl.ds(rows, rows), :],
            send_sem=send_sem.at[k],
            recv_sem=recv_sem.at[k],
            device_id={"wave": other(s)},
            device_id_type=MESH,
        )

    def band_copy(d, c, owner):
        k = lax.rem(c, RING)
        return pltpu.make_async_remote_copy(
            src_ref=ready.at[k, pl.ds(peer(d) * band, band)],
            dst_ref=bands_ref.at[(slice(None), owner, *place(c))],
            send_sem=band_send.at[k, d - 1],
            recv_sem=band_recv.at[c, d - 1],
            device_id={"lev": peer(d)},
            device_id_type=MESH,
        )

    def own_copy(c):
        k = lax.rem(c, RING)
        return pltpu.make_async_copy(
            ready.at[k, pl.ds(lev_pos * band, band)],
            bands_ref.at[(slice(None), lev_pos, *place(c))],
            band_own.at[k],
        )

    def release(s, c):
        @pl.when(c >= RING)
        def _():
            swap(s, c - RING).wait_send()

    def send(s, c):
        @pl.when(c >= RING)
        def _():
            pl.semaphore_wait(free_sem.at[s], 1)

        swap(s, c).start()

    degree = wave_pos * rows + lax.broadcasted_iota(jnp.int32, (rows, lane), 0)

    def begin(c):
        coef_copy(c).wait()
        for n, low in enumerate(range(0, width, lane)):
            part = coef_in[lax.rem(c, 2), :, :, pl.ds(low, lane)].astype(jnp.float32)
            turn[n] = part.reshape(rows * unit, lane)

        @pl.when(c + 2 < chunks)
        def _():
            coef_copy(c + 2).start()

        release(0, c)
        k = slot(0, c)
        for m in range(unit):
            live = degree >= ids_ref[lev_pos * slots + lax.div(c, split) * unit + m]
            for n, low in enumerate(range(0, width, lane)):
                part = turn[n, pl.ds(m, rows, stride=unit), :]
                part = jnp.where(live, part, 0.0)
                mixed[k, m, pl.ds(0, rows), pl.ds(low, lane)] = part.astype(mixed.dtype)
        send(0, c)

    def rearrange(j, low, count):
        s, g = lax.div(lax.rem(j, jobs), groups), lax.rem(j, groups)
        k = lax.rem(j, 2)
        factor_copy(j).wait()
        for o in range(group):
            both = jnp.concatenate(
                [factor_in[k, q, o, :, pl.ds(low, count)] for q in range(2)]
                + [jnp.zeros((2 * lane - 2 * rows, count), factor_in.dtype)],
                axis=0,
            )
            for n in range(2):
                factor_f32[n, pl.ds(o, count, stride=group), :] = (
                    both[n * lane : (n + 1) * lane].T.astype(jnp.float32)
                )

        @pl.when(j + 2 < 2 * jobs)
        def _():
            factor_copy(j + 2).start()

        row = pl.multiple_of(g * group, group)
        for n in range(2):
            factor[pl.ds(s * slots + low, count), pl.ds(row, group), pl.ds(n * lane, lane)] = (
                factor_f32[n, pl.ds(0, count * group), :].astype(factor.dtype).reshape(count, group, lane)
            )

    def prepare(s):
        def job(g, carry):
            rearrange(s * groups + g, 0, front)
            return carry

        lax.fori_loop(0, groups, job, 0)

    def mix(s, c):
        k = slot(s, c)
        swap(s, c).wait_recv()
        last = s == sections - 1
        if last:

            @pl.when(c >= RING)
            def _():
                for d in range(1, lev_count):
                    band_copy(d, c - RING, lev_pos).wait_send()
                own_copy(c - RING).wait()

        else:
            release(s + 1, c)
        for m in range(unit):
            total = jnp.dot(
                factor[s * slots + lax.div(c, split) * unit + m][:, : 2 * rows],
                mixed[k, m],
                preferred_element_type=jnp.float32,
            )
            if last:
                for n, low in enumerate(range(0, width, lane)):
                    turn[n, pl.ds(m, rows, stride=unit), :] = total[:, low : low + lane]
            else:
                mixed[slot(s + 1, c), m, pl.ds(0, rows), :] = total.astype(mixed.dtype)

        @pl.when(c < chunks - RING)
        def _():
            pl.semaphore_signal(free_sem.at[s], inc=1, device_id={"wave": other(s)}, device_id_type=MESH)

        if last:
            for n, low in enumerate(range(0, width, lane)):
                ready[lax.rem(c, RING), :, :, pl.ds(low, lane)] = (
                    turn[n].astype(ready.dtype).reshape(rows, unit, lane)
                )
            for d in (lev_count // 2, 1, lev_count - 1) if lev_count == 4 else range(1, lev_count):
                band_copy(d, c, lev_pos).start()
            own_copy(c).start()
        else:
            send(s + 1, c)

    def guarded(s, c):
        @pl.when((c >= 0) & (c < chunks))
        def _():
            mix(s, c)

    piece = math.gcd(early, slots)
    pieces = slots // piece
    ahead, behind = early * lev_count, (slots - early) * lev_count
    turnover = 2.0 * math.pi / longitudes

    def tabulate(i):
        owner, q = lax.div(i, pieces), lax.rem(i, pieces)
        line = lax.broadcasted_iota(jnp.int32, (piece, lane), 0)
        ids = jnp.zeros((piece, lane), jnp.int32)
        for n in range(piece):
            ids = jnp.where(line == n, ids_ref[owner * slots + q * piece + n], ids)
        j = lax.broadcasted_iota(jnp.int32, ids.shape, 1)
        a = lax.rem(lax.rem(ids * lane, longitudes) * j, longitudes).astype(jnp.float32) * turnover
        b = lax.rem(ids * j, longitudes).astype(jnp.float32) * turnover
        weight = jnp.where(ids == 0, 1.0, 2.0) * (2.0 * slots * lev_count) ** -0.5
        cos_a, sin_a = weight * jnp.cos(a), weight * jnp.sin(a)
        cos_b, sin_b = jnp.cos(b), jnp.sin(b)
        first = q * piece < early
        low = jnp.where(first, owner * early + q * piece, 2 * ahead + (q * piece - early) * lev_count + owner * piece)
        high = low + jnp.where(first, ahead, behind)
        low, high = pl.multiple_of(low, piece), pl.multiple_of(high, piece)
        for n in range(longitudes // lane):
            ca, sa = cos_a[:, n : n + 1], sin_a[:, n : n + 1]
            columns = pl.ds(n * lane, lane)
            table[pl.ds(low, piece), columns] = (ca * cos_b - sa * sin_b).astype(table.dtype)
            table[pl.ds(high, piece), columns] = (-(sa * cos_b + ca * sin_b)).astype(table.dtype)

    later_copy = pltpu.make_async_copy(table.at[pl.ds(2 * ahead, 2 * behind)], later_ref, table_sem)
    tables = lev_count * pieces
    table_at = sections
    table_each = pl.cdiv(tables, early // unit * split - table_at)
    early_chunks = early // unit * split
    rows_at = early_chunks - 1 + RING + sections
    rows_each = pl.cdiv(band, chunks + sections - rows_at)

    def row_copy(r):
        k = lax.rem(r, 2)
        return pltpu.make_async_copy(bands_ref.at[r, :, pl.ds(0, early), :], row_in.at[k], row_sem.at[k])

    def out_copy(r):
        k = lax.rem(r, 2)
        return pltpu.make_async_copy(row_out.at[k], partial_ref.at[r], out_sem.at[k])

    def arrived(c, carry):
        for d in range(1, lev_count):
            band_copy(d, c, peer(lev_count - d)).wait_recv()
        return carry

    def synthesize(r):
        k = lax.rem(r, 2)
        row_copy(r).wait()

        @pl.when(r + 1 < band)
        def _():
            row_copy(r + 1).start()

        @pl.when(r >= 2)
        def _():
            out_copy(r - 2).wait()

        turned = row_in[k].reshape(ahead, channels).T
        spectrum = jnp.concatenate([turned[: channels // 2], turned[channels // 2 :]], axis=1)
        span = math.gcd(longitudes, 512)
        for j in range(0, longitudes, span):
            row_out[k, :, pl.ds(j, span)] = jnp.dot(
                spectrum, table[pl.ds(0, 2 * ahead), pl.ds(j, span)], preferred_element_type=jnp.float32
            ).astype(row_out.dtype)
        out_copy(r).start()

    pl.semaphore_wait(barrier, sections + lev_count - 1)

    def reach(t, jump):
        ahead_of = jnp.where(t > jump, t + 1, t)
        return jnp.minimum(jnp.maximum(ahead_of, 0), chunks)

    def step(t, carry):
        def first(c, carry):
            mix(0, c)
            return carry

        def fresh(c, carry):
            begin(c)
            return carry

        lax.fori_loop(reach(t - 1, 5), reach(t, 5), first, 0)
        lax.fori_loop(reach(t, 5), reach(t + 1, 5), fresh, 0)

        for s in range(1, sections - 1):
            guarded(s, t - 1 - s)

        @pl.when(t < sections)
        def _():
            prepare(t)

        guarded(sections - 1, t - sections)

        @pl.when((t > sections) & (t <= sections + jobs))
        def _():
            rearrange(jobs + t - sections - 1, front, slots - front)

        for n in range(table_each):
            i = (t - table_at) * table_each + n

            @pl.when((i >= 0) & (i < tables))
            def _():
                tabulate(i)

        @pl.when(t == rows_at)
        def _():
            later_copy.start()
            lax.fori_loop(0, early_chunks, arrived, 0)
            row_copy(0).start()

        for n in range(rows_each):
            r = (t - rows_at) * rows_each + n

            @pl.when((r >= 0) & (r < band))
            def _():
                synthesize(r)

        return carry

    lax.fori_loop(0, chunks + sections, step, 0)

    for c in range(chunks - RING, chunks):
        for s in range(sections):
            swap(s, jnp.int32(c)).wait_send()
        for d in range(1, lev_count):
            band_copy(d, jnp.int32(c), lev_pos).wait_send()
        own_copy(jnp.int32(c)).wait()

    lax.fori_loop(early_chunks, chunks, arrived, 0)
    for r in range(band - 2, band):
        out_copy(jnp.int32(r)).wait()
    later_copy.wait()


def exchange(ids, coefficients, factors, unit):
    lev_count = lax.axis_size("lev")
    rows, slots, channels = coefficients.shape
    sections = factors.shape[0]
    chunks = slots // unit * SPLIT
    width = channels // SPLIT
    band = rows // lev_count
    early = EARLY * unit
    kind = coefficients.dtype
    group = 16
    behind = (slots - early) * lev_count
    return pl.pallas_call(
        functools.partial(exchange_kernel, unit, early),
        out_shape=(
            jax.ShapeDtypeStruct((band, lev_count, slots, channels), kind),
            jax.ShapeDtypeStruct((band, channels // 2, NLON), kind),
            jax.ShapeDtypeStruct((2 * behind, NLON), kind),
        ),
        in_specs=[
            pl.BlockSpec(memory_space=pltpu.SMEM),
            pl.BlockSpec(memory_space=pltpu.HBM),
            pl.BlockSpec(memory_space=pltpu.HBM),
        ],
        out_specs=[pl.BlockSpec(memory_space=pltpu.HBM)] * 3,
        scratch_shapes=[
            pltpu.VMEM((2, rows, unit, width), kind),
            pltpu.VMEM((2, 2, group, rows, slots), kind),
            pltpu.VMEM((2, 128 * group, 128), jnp.float32),
            pltpu.VMEM((sections * slots, rows, 256), kind),
            pltpu.VMEM((width // 128, rows * unit, 128), jnp.float32),
            pltpu.VMEM((sections * RING, unit, 2 * rows, width), kind),
            pltpu.VMEM((RING, rows, unit, width), kind),
            pltpu.VMEM((2 * lev_count * slots, NLON), kind),
            pltpu.VMEM((2, lev_count, early, channels), kind),
            pltpu.VMEM((2, channels // 2, NLON), kind),
            pltpu.SemaphoreType.DMA((2,)),
            pltpu.SemaphoreType.DMA((2,)),
            pltpu.SemaphoreType.DMA((sections * RING,)),
            pltpu.SemaphoreType.DMA((sections * RING,)),
            pltpu.SemaphoreType.DMA((RING, lev_count - 1)),
            pltpu.SemaphoreType.DMA((chunks, lev_count - 1)),
            pltpu.SemaphoreType.DMA((RING,)),
            pltpu.SemaphoreType.DMA((2,)),
            pltpu.SemaphoreType.DMA((2,)),
            pltpu.SemaphoreType.DMA,
            pltpu.SemaphoreType.REGULAR((sections,)),
        ],
        compiler_params=pltpu.CompilerParams(
            collective_id=0, has_side_effects=True, vmem_limit_bytes=60 << 20
        ),
    )(ids, coefficients, factors)


def finish_kernel(count, *refs):
    partial_ref, table_ref, out_ref = refs[count:]
    tall, half, longitudes = out_ref.shape
    channels = refs[0].shape[3]
    lines = []
    for r in range(tall):
        wide = jnp.concatenate([ref[r].reshape(-1, channels) for ref in refs[:count]], axis=0)
        turned = wide.T
        lines.append(jnp.concatenate([turned[:half], turned[half:]], axis=1))
    spectrum = jnp.concatenate(lines, axis=0)
    span = math.gcd(longitudes, 512)
    for j in range(0, longitudes, span):
        total = jnp.dot(spectrum, table_ref[:, j : j + span], preferred_element_type=jnp.float32)
        for r in range(tall):
            own = total[r * half : (r + 1) * half] + partial_ref[r, :, j : j + span].astype(jnp.float32)
            out_ref[r, :, j : j + span] = own.astype(out_ref.dtype)


def finish(bands, partial, table, early):
    rows, owners, slots, channels = bands.shape
    tall = math.gcd(rows, TALL)
    piece = math.gcd(early, slots)
    starts = range(early // piece, slots // piece)
    whole_row = pl.BlockSpec((tall, *partial.shape[1:]), lambda i: (i, 0, 0))
    return pl.pallas_call(
        functools.partial(finish_kernel, len(starts)),
        grid=(rows // tall,),
        out_shape=jax.ShapeDtypeStruct(partial.shape, partial.dtype),
        in_specs=[pl.BlockSpec((tall, owners, piece, channels), lambda i, n=n: (i, 0, n, 0)) for n in starts]
        + [whole_row, pl.BlockSpec(table.shape, lambda i: (0, 0), pipeline_mode=pl.Buffered(1))],
        out_specs=whole_row,
        cost_estimate=pl.CostEstimate(
            flops=2 * partial.size * table.shape[0],
            bytes_accessed=2 * (2 * partial.size + table.size),
            transcendentals=0,
        ),
    )(*[bands] * len(starts), partial, table)


def unit_of(rows, slots):
    return UNIT if rows % 16 == 0 and 128 <= 2 * rows <= 256 and 128 < slots <= 256 and slots % UNIT == 0 and slots // UNIT > EARLY + RING else 0


def staged(coefficients, factors, wave_ids):
    rows, slots, _ = coefficients.shape
    unit = unit_of(rows, slots)
    bands, partial, table = exchange(wave_ids, coefficients, factors, unit)
    return finish(bands, partial, table, EARLY * unit)


def solution(mesh):
    in_specs = (P("wave", "lev", None), P(None, None, "wave", None, "lev"), P())
    out_specs = P(("wave", "lev"), None, None)

    def mapped(step):
        return jax.shard_map(step, mesh=mesh, in_specs=in_specs, out_specs=out_specs, check_vma=False)

    def run(coefficients, factors, wave_ids):
        lev_count = mesh.shape["lev"]
        slots = coefficients.shape[1] // lev_count
        if unit_of(factors.shape[3], slots):
            return mapped(staged)(coefficients, factors, wave_ids)
        return mapped(whole)(coefficients, factors, wave_ids)

    return run
```
